32 devices in a mesh: shard: 16 (over z, x, core), rep: 2 (over y).
Axes of the slice: x: 2, y: 2, z: 4, core: 2. Of those that a mesh axis runs over, the one named last changes fastest.
Arguments:
- frames: bfloat16 [32, 256, 768], P(('shard', 'rep')), may hold values from -6 to 6
- cotangent: bfloat16 [32, 256, 768], P(('shard', 'rep')), may hold values from -6 to 6
- first_gain: bfloat16 [768], P('shard'), may hold values from 0.5 to 1.5
- first_shift: bfloat16 [768], P('shard'), may hold values from -1.75 to 1.75
- query_weight: bfloat16 [768, 768], P('shard'), may hold values from -0.21875 to 0.21875
- query_bias: bfloat16 [768], P('shard'), may hold values from -1.75 to 1.75
- key_weight: bfloat16 [768, 768], P('shard'), may hold values from -0.21875 to 0.21875
- value_weight: bfloat16 [768, 768], P('shard'), may hold values from -0.21875 to 0.21875
- value_bias: bfloat16 [768], P('shard'), may hold values from -1.75 to 1.75
- output_weight: bfloat16 [768, 768], P('shard'), may hold values from -0.4375 to 0.4375
- output_bias: bfloat16 [768], P('shard'), may hold values from -1.75 to 1.75
- second_gain: bfloat16 [768], P('shard'), may hold values from 0.5 to 1.5
- second_shift: bfloat16 [768], P('shard'), may hold values from -1.75 to 1.75
- inner_weight: bfloat16 [768, 3072], P('shard'), may hold values from -0.21875 to 0.21875
- inner_bias: bfloat16 [3072], P('shard'), may hold values from -1.75 to 1.75
- outer_weight: bfloat16 [3072, 768], P('shard'), may hold values from -0.109375 to 0.109375
- outer_bias: bfloat16 [768], P('shard'), may hold values from -1.75 to 1.75
Outputs:
- result: bfloat16 [32, 256, 768], P(('shard', 'rep'))
- input_grad: bfloat16 [32, 256, 768], P(('shard', 'rep'))
- grad_first_gain: float32 [768], P('shard')
- grad_first_shift: float32 [768], P('shard')
- grad_query_weight: float32 [768, 768], P('shard')
- grad_query_bias: float32 [768], P('shard')
- grad_key_weight: float32 [768, 768], P('shard')
- grad_value_weight: float32 [768, 768], P('shard')
- grad_value_bias: float32 [768], P('shard')
- grad_output_weight: float32 [768, 768], P('shard')
- grad_output_bias: float32 [768], P('shard')
- grad_second_gain: float32 [768], P('shard')
- grad_second_shift: float32 [768], P('shard')
- grad_inner_weight: float32 [768, 3072], P('shard')
- grad_inner_bias: float32 [3072], P('shard')
- grad_outer_weight: float32 [3072, 768], P('shard')
- grad_outer_bias: float32 [768], P('shard')
The draws below stay inside these ranges and needn't reach their ends.
All inputs are finite; a program needn't handle non-finite values.
Results may differ from the reference program's by a relative error of at most 0.019.
Values may be sent and summed in bfloat16 or wider, within the bound.
A program may use at most 128 MiB of HBM per device.

```python
import jax
import jax.numpy as jnp
from jax import lax

D = 768
HEADS = 12
HD = 64
FF = 3072
FRAMES = 256
CLIPS = 32


def with_spikes(values, rng, source, target, blocks, factor):
    def block_of(position):
        return (jnp.arange(values.shape[position]) // (values.shape[position] // blocks)).reshape((-1,) + (1,) * (values.ndim - 1 - position))

    one_side = jax.random.permutation(rng, blocks)[block_of(target)]
    other_side = (block_of(target) + blocks // 2) % blocks
    return jnp.where((block_of(source) == one_side) | (block_of(source) == other_side), factor * values, values)


def levels(key, extent, pieces, smallest, high):
    def one(axis_at, blocks):
        steps = jax.random.uniform(jax.random.fold_in(jax.random.fold_in(key, 6), axis_at), (blocks,), jnp.float32, smallest / len(pieces), high / len(pieces))
        return jnp.repeat(jnp.exp(steps), extent[axis_at] // blocks).reshape((-1,) + (1,) * (len(extent) - axis_at - 1))

    loudness = one(*pieces[0])
    for cut in pieces[1:]:
        loudness = loudness * one(*cut)
    return loudness


def centred(own_key, extent, width, bound, split=(), held_as=jnp.bfloat16):
    drawn = width * jax.random.normal(own_key, extent, jnp.float32)
    if split:
        drawn = drawn * levels(own_key, extent, split, -0.22, 0.18)
    return jnp.clip(drawn, -bound, bound).astype(held_as)


def bell_draw_with(own_key, shape, scale, reach, split, heavy, held_as=jnp.bfloat16):
    entries = scale * jax.random.normal(own_key, shape, jnp.float32)
    if split:
        entries = entries * levels(own_key, shape, split, -0.22, 0.18)
    return jnp.clip(with_spikes(entries, jax.random.fold_in(own_key, 3), *heavy), -reach, reach).astype(held_as)


def setup_inputs(seed: int = 0) -> dict:
    streams_of = jax.random.split(jax.random.key(seed), 18)
    return {
        "frames": bell_draw_with(streams_of[0], (CLIPS, FRAMES, D), 1.0, 6.0, ((0, 32),), (0, 2, 32, 2.75)),
        "cotangent": centred(streams_of[1], (CLIPS, FRAMES, D), 1.0, 6.0, ((0, 32),)),
        "first_gain": jnp.clip(1.0 + 0.1 * jax.random.normal(streams_of[2], (D,), jnp.float32), 0.5, 1.5).astype(jnp.bfloat16),
        "first_shift": centred(streams_of[3], (D,), 0.3, 1.75, ((0, 16),)),
        "query_weight": centred(streams_of[4], (D, D), D ** -0.5, 0.21875, ((0, 16),)),
        "query_bias": centred(streams_of[5], (D,), 0.3, 1.75, ((0, 16),)),
        "key_weight": centred(streams_of[6], (D, D), D ** -0.5, 0.21875, ((0, 16),)),
        "value_weight": centred(streams_of[7], (D, D), D ** -0.5, 0.21875, ((0, 16),)),
        "value_bias": centred(streams_of[8], (D,), 0.3, 1.75, ((0, 16),)),
        "output_weight": centred(streams_of[9], (D, D), (D // 4) ** -0.5, 0.4375, ((0, 16),)),
        "output_bias": centred(streams_of[10], (D,), 0.3, 1.75, ((0, 16),)),
        "second_gain": jnp.clip(1.0 + 0.1 * jax.random.normal(streams_of[11], (D,), jnp.float32), 0.5, 1.5).astype(jnp.bfloat16),
        "second_shift": centred(streams_of[12], (D,), 0.3, 1.75, ((0, 16),)),
        "inner_weight": centred(streams_of[13], (D, FF), D ** -0.5, 0.21875, ((0, 16),)),
        "inner_bias": centred(streams_of[14], (FF,), 0.3, 1.75, ((0, 16),)),
        "outer_weight": centred(streams_of[15], (FF, D), FF ** -0.5, 0.109375, ((0, 16),)),
        "outer_bias": centred(streams_of[16], (D,), 0.3, 1.75, ((0, 16),)),
    }


EPSILON = 1e-05

def normalize(values, gain, shift):
    center = lax.optimization_barrier(jnp.mean(values, axis=-1, keepdims=True))
    spread = lax.optimization_barrier(jnp.mean((values - center) ** 2, axis=-1, keepdims=True))
    inv_std = lax.rsqrt(spread + EPSILON)
    normed = (values - center) * inv_std
    return (normed * gain.astype(jnp.float32) + shift.astype(jnp.float32), normed, inv_std)

def norm_back(grad_out, normed, inv_std, gain):
    scaled = grad_out * gain.astype(jnp.float32)
    return inv_std * (scaled - lax.optimization_barrier(jnp.mean(scaled, axis=-1, keepdims=True)) - normed * lax.optimization_barrier(jnp.mean(scaled * normed, axis=-1, keepdims=True)))

def gelu_parts(inner):
    cdf = 0.5 * (1.0 + jax.scipy.special.erf(inner * 0.7071067811865476))
    density = jnp.exp(-0.5 * inner * inner) * 0.3989422804014327
    return (inner * cdf, cdf + inner * density)

def heads_of(matrix):
    return matrix.reshape(matrix.shape[0], HEADS, HD).astype(jnp.float32)

def matmul(left, right):
    return jnp.dot(left, right, preferred_element_type=jnp.float32)

def forward_clip(clip, params):
    first_gain, first_shift, query_weight, query_bias, key_weight, value_weight, value_bias, output_weight, output_bias, second_gain, second_shift, inner_weight, inner_bias, outer_weight, outer_bias = params
    start = clip.astype(jnp.float32)
    normed_one, hat_one, inv_one = normalize(start, first_gain, first_shift)
    first_low = normed_one.astype(jnp.bfloat16)
    query = ((matmul(first_low, query_weight) + query_bias.astype(jnp.float32)) * HD ** (-0.5)).astype(jnp.bfloat16)
    keys = matmul(first_low, key_weight).astype(jnp.bfloat16)
    values = (matmul(first_low, value_weight) + value_bias.astype(jnp.float32)).astype(jnp.bfloat16)
    scores = jnp.einsum('qhd,khd->hqk', heads_of(query), heads_of(keys))
    highest = lax.optimization_barrier(jnp.max(scores, axis=-1, keepdims=True))
    log_total = highest + jnp.log(lax.optimization_barrier(jnp.sum(jnp.exp(scores - highest), axis=-1, keepdims=True)))
    probs = jnp.exp(scores - log_total).astype(jnp.bfloat16)
    context = jnp.einsum('hqk,khd->qhd', probs.astype(jnp.float32), heads_of(values)).reshape(-1, D).astype(jnp.bfloat16)
    mixed = start + matmul(context, output_weight) + output_bias.astype(jnp.float32)
    normed_two, hat_two, inv_two = normalize(mixed, second_gain, second_shift)
    second_low = normed_two.astype(jnp.bfloat16)
    inner = matmul(second_low, inner_weight) + inner_bias.astype(jnp.float32)
    active, slope = gelu_parts(inner)
    active_low = active.astype(jnp.bfloat16)
    result = (mixed + matmul(active_low, outer_weight) + outer_bias.astype(jnp.float32)).astype(jnp.bfloat16)
    saved = (hat_one, inv_one, first_low, query, keys, values, log_total, context, hat_two, inv_two, second_low, slope, active_low)
    return (result, saved)

def backward_clip(grad_low, saved, params):
    first_gain, first_shift, query_weight, query_bias, key_weight, value_weight, value_bias, output_weight, output_bias, second_gain, second_shift, inner_weight, inner_bias, outer_weight, outer_bias = params
    hat_one, inv_one, first_low, query, keys, values, log_total, context, hat_two, inv_two, second_low, slope, active_low = saved
    grad = grad_low.astype(jnp.float32)
    g_outer_bias = lax.optimization_barrier(jnp.sum(grad, axis=0))
    g_outer = matmul(active_low.T, grad_low)
    d_inner = matmul(grad_low, outer_weight.T) * slope
    d_inner_low = d_inner.astype(jnp.bfloat16)
    g_inner_bias = lax.optimization_barrier(jnp.sum(d_inner, axis=0))
    g_inner = matmul(second_low.T, d_inner_low)
    d_second = matmul(d_inner_low, inner_weight.T)
    g_second_gain = lax.optimization_barrier(jnp.sum(d_second * hat_two, axis=0))
    g_second_shift = lax.optimization_barrier(jnp.sum(d_second, axis=0))
    d_mixed = grad + norm_back(d_second, hat_two, inv_two, second_gain)
    d_mixed_low = d_mixed.astype(jnp.bfloat16)
    g_output_bias = lax.optimization_barrier(jnp.sum(d_mixed, axis=0))
    g_output = matmul(context.T, d_mixed_low)
    d_context = matmul(d_mixed_low, output_weight.T).astype(jnp.bfloat16)
    query_heads = heads_of(query)
    keys_heads = heads_of(keys)
    values_heads = heads_of(values)
    dctx_heads = heads_of(d_context)
    scores = jnp.einsum('qhd,khd->hqk', query_heads, keys_heads)
    probs = jnp.exp(scores - log_total)
    probs_low = probs.astype(jnp.bfloat16).astype(jnp.float32)
    d_probs = jnp.einsum('qhd,khd->hqk', dctx_heads, values_heads)
    delta = lax.optimization_barrier(jnp.sum(dctx_heads * heads_of(context), axis=-1))
    d_scores = (probs * (d_probs - jnp.transpose(delta)[:, :, None])).astype(jnp.bfloat16).astype(jnp.float32)
    d_values = jnp.einsum('hqk,qhd->khd', probs_low, dctx_heads).reshape(-1, D)
    d_query = jnp.einsum('hqk,khd->qhd', d_scores, keys_heads).reshape(-1, D) * HD ** (-0.5)
    d_keys = jnp.einsum('hqk,qhd->khd', d_scores, query_heads).reshape(-1, D)
    dq_low = d_query.astype(jnp.bfloat16)
    dk_low = d_keys.astype(jnp.bfloat16)
    dv_low = d_values.astype(jnp.bfloat16)
    g_query_bias = lax.optimization_barrier(jnp.sum(d_query, axis=0))
    g_value_bias = lax.optimization_barrier(jnp.sum(d_values, axis=0))
    g_query = matmul(first_low.T, dq_low)
    g_keys = matmul(first_low.T, dk_low)
    g_values = matmul(first_low.T, dv_low)
    d_first = matmul(dq_low, query_weight.T) + matmul(dk_low, key_weight.T) + matmul(dv_low, value_weight.T)
    g_first_gain = lax.optimization_barrier(jnp.sum(d_first * hat_one, axis=0))
    g_first_shift = lax.optimization_barrier(jnp.sum(d_first, axis=0))
    d_start = (d_mixed + norm_back(d_first, hat_one, inv_one, first_gain)).astype(jnp.bfloat16)
    grads = (g_first_gain, g_first_shift, g_query, g_query_bias, g_keys, g_values, g_value_bias, g_output, g_output_bias, g_second_gain, g_second_shift, g_inner, g_inner_bias, g_outer, g_outer_bias)
    return (d_start, grads)

def reference(frames, cotangent, first_gain, first_shift, query_weight, query_bias, key_weight, value_weight, value_bias, output_weight, output_bias, second_gain, second_shift, inner_weight, inner_bias, outer_weight, outer_bias):
    params = (first_gain, first_shift, query_weight, query_bias, key_weight, value_weight, value_bias, output_weight, output_bias, second_gain, second_shift, inner_weight, inner_bias, outer_weight, outer_bias)

    def one_clip(totals, pair):
        clip, grad_low = pair
        result, saved = forward_clip(clip, params)
        d_start, grads = backward_clip(grad_low, saved, params)
        return (tuple((total + piece for total, piece in zip(totals, grads))), (result, d_start))
    zeros = tuple((jnp.zeros(weight.shape, jnp.float32) for weight in params))
    totals, (results, input_grad) = lax.scan(one_clip, zeros, (frames, cotangent))
    return (results, input_grad, totals[0], totals[1], totals[2], totals[3], totals[4], totals[5], totals[6], totals[7], totals[8], totals[9], totals[10], totals[11], totals[12], totals[13], totals[14])
```

```python
import functools

import jax
import jax.numpy as jnp
from jax import lax
from jax.experimental import pallas as pl
from jax.experimental.pallas import tpu as pltpu
from jax.sharding import PartitionSpec as P

D = 768
HEADS = 12
HD = 64


EPSILON = 1e-05


def normalize(values, gain, shift):
    center = jnp.mean(values, axis=-1, keepdims=True)
    spread = jnp.mean((values - center) ** 2, axis=-1, keepdims=True)
    inv_std = lax.rsqrt(spread + EPSILON)
    normed = (values - center) * inv_std
    return (normed * gain.astype(jnp.float32) + shift.astype(jnp.float32), normed, inv_std)


def norm_back(grad_out, normed, inv_std, gain):
    scaled = grad_out * gain.astype(jnp.float32)
    return inv_std * (
        scaled
        - jnp.mean(scaled, axis=-1, keepdims=True)
        - normed * jnp.mean(scaled * normed, axis=-1, keepdims=True)
    )


def gelu_parts(inner):
    cdf = 0.5 * (1.0 + jax.scipy.special.erf(inner * 0.7071067811865476))
    density = jnp.exp(-0.5 * inner * inner) * 0.3989422804014327
    return (inner * cdf, cdf + inner * density)


def heads_of(matrix):
    return matrix.reshape(matrix.shape[0], HEADS, HD)


def matmul(left, right):
    return jnp.dot(left, right, preferred_element_type=jnp.float32)


def forward_clip(clip, params):
    (
        first_gain,
        first_shift,
        query_weight,
        query_bias,
        key_weight,
        value_weight,
        value_bias,
        output_weight,
        output_bias,
        second_gain,
        second_shift,
        inner_weight,
        inner_bias,
        outer_weight,
        outer_bias,
    ) = params
    start = clip.astype(jnp.float32)
    normed_one, hat_one, inv_one = normalize(start, first_gain, first_shift)
    first_low = normed_one.astype(jnp.bfloat16)
    query = (
        (matmul(first_low, query_weight) + query_bias.astype(jnp.float32)) * HD ** (-0.5)
    ).astype(jnp.bfloat16)
    keys = matmul(first_low, key_weight).astype(jnp.bfloat16)
    values = (matmul(first_low, value_weight) + value_bias.astype(jnp.float32)).astype(jnp.bfloat16)
    scores = jnp.einsum(
        "qhd,khd->hqk", heads_of(query), heads_of(keys), preferred_element_type=jnp.float32
    )
    highest = jnp.max(scores, axis=-1, keepdims=True)
    log_total = highest + jnp.log(jnp.sum(jnp.exp(scores - highest), axis=-1, keepdims=True))
    probs = jnp.exp(scores - log_total).astype(jnp.bfloat16)
    context = (
        jnp.einsum("hqk,khd->qhd", probs, heads_of(values), preferred_element_type=jnp.float32)
        .reshape(-1, D)
        .astype(jnp.bfloat16)
    )
    mixed = start + matmul(context, output_weight) + output_bias.astype(jnp.float32)
    normed_two, hat_two, inv_two = normalize(mixed, second_gain, second_shift)
    second_low = normed_two.astype(jnp.bfloat16)
    inner = matmul(second_low, inner_weight) + inner_bias.astype(jnp.float32)
    active, slope = gelu_parts(inner)
    active_low = active.astype(jnp.bfloat16)
    result = (mixed + matmul(active_low, outer_weight) + outer_bias.astype(jnp.float32)).astype(
        jnp.bfloat16
    )
    saved = (
        hat_one,
        inv_one,
        first_low,
        query,
        keys,
        values,
        log_total,
        context,
        hat_two,
        inv_two,
        second_low,
        slope,
        active_low,
    )
    return (result, saved)


def backward_clip(grad_low, saved, params):
    (
        first_gain,
        first_shift,
        query_weight,
        query_bias,
        key_weight,
        value_weight,
        value_bias,
        output_weight,
        output_bias,
        second_gain,
        second_shift,
        inner_weight,
        inner_bias,
        outer_weight,
        outer_bias,
    ) = params
    (
        hat_one,
        inv_one,
        first_low,
        query,
        keys,
        values,
        log_total,
        context,
        hat_two,
        inv_two,
        second_low,
        slope,
        active_low,
    ) = saved
    grad = grad_low.astype(jnp.float32)
    g_outer_bias = jnp.sum(grad, axis=0)
    g_outer = matmul(active_low.T, grad_low)
    d_inner = matmul(grad_low, outer_weight.T) * slope
    d_inner_low = d_inner.astype(jnp.bfloat16)
    g_inner_bias = jnp.sum(d_inner, axis=0)
    g_inner = matmul(second_low.T, d_inner_low)
    d_second = matmul(d_inner_low, inner_weight.T)
    g_second_gain = jnp.sum(d_second * hat_two, axis=0)
    g_second_shift = jnp.sum(d_second, axis=0)
    d_mixed = grad + norm_back(d_second, hat_two, inv_two, second_gain)
    d_mixed_low = d_mixed.astype(jnp.bfloat16)
    g_output_bias = jnp.sum(d_mixed, axis=0)
    g_output = matmul(context.T, d_mixed_low)
    d_context = matmul(d_mixed_low, output_weight.T).astype(jnp.bfloat16)
    query_heads = heads_of(query)
    keys_heads = heads_of(keys)
    values_heads = heads_of(values)
    dctx_heads = heads_of(d_context)
    scores = jnp.einsum("qhd,khd->hqk", query_heads, keys_heads, preferred_element_type=jnp.float32)
    probs = jnp.exp(scores - log_total)
    probs_low = probs.astype(jnp.bfloat16)
    d_probs = jnp.einsum(
        "qhd,khd->hqk", dctx_heads, values_heads, preferred_element_type=jnp.float32
    )
    delta = jnp.sum(dctx_heads.astype(jnp.float32) * heads_of(context).astype(jnp.float32), axis=-1)
    d_scores = (probs * (d_probs - jnp.transpose(delta)[:, :, None])).astype(jnp.bfloat16)
    d_values = jnp.einsum(
        "hqk,qhd->khd", probs_low, dctx_heads, preferred_element_type=jnp.float32
    ).reshape(-1, D)
    d_query = jnp.einsum(
        "hqk,khd->qhd", d_scores, keys_heads, preferred_element_type=jnp.float32
    ).reshape(-1, D) * HD ** (-0.5)
    d_keys = jnp.einsum(
        "hqk,qhd->khd", d_scores, query_heads, preferred_element_type=jnp.float32
    ).reshape(-1, D)
    dq_low = d_query.astype(jnp.bfloat16)
    dk_low = d_keys.astype(jnp.bfloat16)
    dv_low = d_values.astype(jnp.bfloat16)
    g_query_bias = jnp.sum(d_query, axis=0)
    g_value_bias = jnp.sum(d_values, axis=0)
    g_query = matmul(first_low.T, dq_low)
    g_keys = matmul(first_low.T, dk_low)
    g_values = matmul(first_low.T, dv_low)
    d_first = (
        matmul(dq_low, query_weight.T)
        + matmul(dk_low, key_weight.T)
        + matmul(dv_low, value_weight.T)
    )
    g_first_gain = jnp.sum(d_first * hat_one, axis=0)
    g_first_shift = jnp.sum(d_first, axis=0)
    d_start = (d_mixed + norm_back(d_first, hat_one, inv_one, first_gain)).astype(jnp.bfloat16)
    grads = (
        g_first_gain,
        g_first_shift,
        g_query,
        g_query_bias,
        g_keys,
        g_values,
        g_value_bias,
        g_output,
        g_output_bias,
        g_second_gain,
        g_second_shift,
        g_inner,
        g_inner_bias,
        g_outer,
        g_outer_bias,
    )
    return (d_start, grads)


MESH = pl.DeviceIdType.MESH


class Ring:
    def __init__(self, chips):
        self.chips = chips
        shard = lax.axis_index("shard")
        self.rep = lax.axis_index("rep")
        self.core = lax.rem(shard, 2)
        chip = shard // 2
        half = chip // 2
        self.pos = half + lax.rem(chip, 2) * (chips - 1 - 2 * half)
        self.step = 1 - 2 * self.core
        self.me = shard
        self.mate = chip * 2 + (1 - self.core)

    def shard_at(self, offset, core):
        place = lax.rem(self.pos + offset + 2 * self.chips, self.chips)
        far = place // (self.chips // 2)
        chip = (1 - far) * 2 * place + far * (2 * (self.chips - 1 - place) + 1)
        return chip * 2 + core

    def next(self):
        return self.shard_at(self.step, self.core)

    def previous(self):
        return self.shard_at(-self.step, self.core)


def rows_of(owner, rows):
    return pl.ds(pl.multiple_of(owner * rows, rows), rows)


def greet(ring, others, reps):
    barrier = pltpu.get_barrier_semaphore()
    for other in others:
        pl.semaphore_signal(barrier, inc=1, device_id=(other, ring.rep), device_id_type=MESH)
    for shift in range(1, reps):
        pl.semaphore_signal(
            barrier,
            inc=1,
            device_id=(ring.me, lax.rem(ring.rep + shift, reps)),
            device_id_type=MESH,
        )
    pl.semaphore_wait(barrier, len(others) + reps - 1)


def gather_kernel(chips, count, *refs):
    ins, outs = refs[:count], refs[count : 2 * count]
    ring_send, ring_recv, mate_send, mate_recv, own_sem = refs[2 * count :]
    ring = Ring(chips)
    core = ring.core
    following, mate = ring.next(), ring.mate
    greet(ring, (following, ring.previous(), mate), 1)

    def where(index, owner):
        return outs[index].at[rows_of(owner, ins[index].shape[0])]

    def to_next(index, step, owner, source):
        return pltpu.make_async_remote_copy(
            src_ref=source,
            dst_ref=where(index, owner),
            send_sem=ring_send.at[step, index],
            recv_sem=ring_recv.at[step, index],
            device_id=(following, ring.rep),
            device_id_type=MESH,
        )

    def to_mate(index, step, owner, source):
        return pltpu.make_async_remote_copy(
            src_ref=source,
            dst_ref=where(index, owner),
            send_sem=mate_send.at[step, index],
            recv_sem=mate_recv.at[step, index],
            device_id=(mate, ring.rep),
            device_id_type=MESH,
        )

    for index in range(count):
        to_next(index, 0, ring.me, ins[index]).start()
    for index in range(count):
        to_mate(index, 0, ring.me, ins[index]).start()
        pltpu.make_async_copy(ins[index], where(index, ring.me), own_sem.at[index]).start()

    def hop(step, carry):
        owner = ring.shard_at(-ring.step * step, core)
        for index in range(count):
            block = where(index, owner)
            to_next(index, step - 1, owner, block).wait_recv()
            pl.when(step < chips - 1)(lambda: to_next(index, step, owner, block).start())
            to_mate(index, step, owner, block).start()
        return carry

    lax.fori_loop(1, chips, hop, 0)

    def finish(step, carry):
        owner = ring.shard_at(-ring.step * step, core)
        theirs = ring.shard_at(ring.step * step, 1 - core)
        for index in range(count):
            to_mate(index, step, theirs, where(index, theirs)).wait_recv()
            to_mate(index, step, owner, where(index, owner)).wait_send()
            pl.when(step < chips - 1)(
                lambda: to_next(index, step, owner, where(index, owner)).wait_send()
            )
        return carry

    lax.fori_loop(0, chips, finish, 0)
    for index in range(count):
        pltpu.make_async_copy(ins[index], where(index, ring.me), own_sem.at[index]).wait()


def gather_all(pieces, shards):
    chips, count = shards // 2, len(pieces)
    return pl.pallas_call(
        functools.partial(gather_kernel, chips, count),
        out_shape=[
            jax.ShapeDtypeStruct((piece.shape[0] * shards, piece.shape[1]), piece.dtype)
            for piece in pieces
        ],
        in_specs=[pl.BlockSpec(memory_space=pltpu.VMEM)] * count,
        out_specs=[pl.BlockSpec(memory_space=pl.ANY)] * count,
        scratch_shapes=[
            pltpu.SemaphoreType.DMA((chips, count)),
            pltpu.SemaphoreType.DMA((chips, count)),
            pltpu.SemaphoreType.DMA((chips, count)),
            pltpu.SemaphoreType.DMA((chips, count)),
            pltpu.SemaphoreType.DMA((count,)),
        ],
        compiler_params=pltpu.CompilerParams(collective_id=0, has_side_effects=True),
        name="gather_all",
    )(*pieces)


def scatter_kernel(chips, reps, count, *refs):
    ins, outs = refs[:count], refs[count : 2 * count]
    held = refs[2 * count : 3 * count]
    arrived = refs[3 * count : 4 * count]
    peers = refs[4 * count : 5 * count]
    ring_send, ring_recv, mate_send, mate_recv, rep_send, rep_recv = refs[5 * count :]
    ring = Ring(chips)
    core = ring.core
    following, mate = ring.next(), ring.mate
    greet(ring, (following, ring.previous(), mate), reps)

    def to_mate(index, step):
        owner = ring.shard_at(ring.step * (step + 1), 1 - core)
        rows = outs[index].shape[0]
        return pltpu.make_async_remote_copy(
            src_ref=ins[index].at[rows_of(owner, rows)],
            dst_ref=held[index].at[step],
            send_sem=mate_send.at[step, index],
            recv_sem=mate_recv.at[step, index],
            device_id=(mate, ring.rep),
            device_id_type=MESH,
        )

    def to_next(index, step):
        return pltpu.make_async_remote_copy(
            src_ref=held[index].at[step],
            dst_ref=arrived[index].at[step],
            send_sem=ring_send.at[step, index],
            recv_sem=ring_recv.at[step, index],
            device_id=(following, ring.rep),
            device_id_type=MESH,
        )

    def to_rep(index, shift):
        return pltpu.make_async_remote_copy(
            src_ref=held[index].at[chips - 1],
            dst_ref=peers[index].at[ring.rep],
            send_sem=rep_send.at[shift, index],
            recv_sem=rep_recv.at[shift, index],
            device_id=(ring.me, lax.rem(ring.rep + shift, reps)),
            device_id_type=MESH,
        )

    def hand_over(step, carry):
        for index in range(count):
            to_mate(index, step).start()
        return carry

    lax.fori_loop(0, chips, hand_over, 0)

    def add(index, step, first):
        owner = ring.shard_at(-ring.step * (step + 1), core)
        rows = outs[index].shape[0]
        to_mate(index, step).wait_recv()
        total = ins[index][rows_of(owner, rows), :].astype(jnp.float32) + held[index][step].astype(
            jnp.float32
        )
        if not first:
            to_next(index, step - 1).wait_recv()
            total = total + arrived[index][step - 1].astype(jnp.float32)
        held[index][step] = total.astype(jnp.bfloat16)

    for index in range(count):
        add(index, 0, True)
        to_next(index, 0).start()

    def hop(step, carry):
        for index in range(count):
            add(index, step, False)
            to_next(index, step).start()
        return carry

    lax.fori_loop(1, chips - 1, hop, 0)
    for index in range(count):
        add(index, chips - 1, False)
        for shift in range(1, reps):
            to_rep(index, shift).start()
        peers[index][ring.rep] = held[index][chips - 1]
    for index in range(count):
        for shift in range(1, reps):
            to_rep(index, shift).wait_recv()
        total = peers[index][0].astype(jnp.float32)
        for rep in range(1, reps):
            total = total + peers[index][rep].astype(jnp.float32)
        outs[index][...] = total

    def finish(step, carry):
        for index in range(count):
            to_mate(index, step).wait_send()
            pl.when(step < chips - 1)(lambda: to_next(index, step).wait_send())
        return carry

    lax.fori_loop(0, chips, finish, 0)
    for index in range(count):
        for shift in range(1, reps):
            to_rep(index, shift).wait_send()


def scatter_all(pieces, shards, reps):
    chips, count = shards // 2, len(pieces)
    blocks = [(piece.shape[0] // shards, piece.shape[1]) for piece in pieces]
    return pl.pallas_call(
        functools.partial(scatter_kernel, chips, reps, count),
        out_shape=[jax.ShapeDtypeStruct(block, jnp.float32) for block in blocks],
        in_specs=[pl.BlockSpec(memory_space=pltpu.VMEM)] * count,
        out_specs=[pl.BlockSpec(memory_space=pltpu.VMEM)] * count,
        scratch_shapes=[pltpu.VMEM((chips,) + block, jnp.bfloat16) for block in blocks]
        + [pltpu.VMEM((chips - 1,) + block, jnp.bfloat16) for block in blocks]
        + [pltpu.VMEM((reps,) + block, jnp.bfloat16) for block in blocks]
        + [pltpu.SemaphoreType.DMA((chips, count))] * 4
        + [pltpu.SemaphoreType.DMA((reps, count))] * 2,
        compiler_params=pltpu.CompilerParams(
            collective_id=1, has_side_effects=True, vmem_limit_bytes=60 * 1024 * 1024
        ),
        name="scatter_all",
    )(*pieces)


NARROW = (0, 1, 3, 6, 8, 9, 10, 14)
WIDE = 12
WEIGHTS = (2, 4, 5, 7, 11, 13)
LANES = 128
SUBLANES = 16


def packed_rows(size):
    return -(-size // (LANES * SUBLANES)) * SUBLANES


def pack(vectors, owners):
    flat = jnp.concatenate(
        [vectors[i].reshape(owners, -1) for i in NARROW] + [vectors[WIDE].reshape(owners, -1)],
        axis=1,
    )
    rows = packed_rows(flat.shape[1])
    flat = jnp.pad(flat, ((0, 0), (0, rows * LANES - flat.shape[1])))
    return flat.reshape(owners * rows, LANES)


def unpack(block, owners, narrow, wide):
    flat = block.reshape(owners, -1)
    count = len(NARROW)
    first = flat[:, : count * narrow].reshape(owners, count, narrow)
    first = jnp.transpose(first, (1, 0, 2)).reshape(count, owners * narrow)
    found = {i: first[k] for k, i in enumerate(NARROW)}
    found[WIDE] = flat[:, count * narrow : count * narrow + wide].reshape(-1)
    return found


def per_device(shards, reps, frames, cotangent, *local):
    narrow, wide = local[0].shape[0], local[WIDE].shape[0]
    gathered = gather_all([local[i] for i in WEIGHTS] + [pack(local, 1)], shards)
    params = [None] * len(local)
    for k, i in enumerate(WEIGHTS):
        params[i] = gathered[k]
    for i, vector in unpack(gathered[-1], shards, narrow, wide).items():
        params[i] = vector
    params = tuple(params)

    results, input_grads, totals = [], [], None
    for k in range(frames.shape[0]):
        result, saved = forward_clip(frames[k], params)
        d_start, grads = backward_clip(cotangent[k], saved, params)
        results.append(result)
        input_grads.append(d_start)
        totals = grads if totals is None else tuple(a + b for a, b in zip(totals, grads))

    low = [total.astype(jnp.bfloat16) for total in totals]
    summed = scatter_all([low[i] for i in WEIGHTS] + [pack(low, shards)], shards, reps)
    out = [None] * len(local)
    for k, i in enumerate(WEIGHTS):
        out[i] = summed[k]
    for i, vector in unpack(summed[-1], 1, narrow, wide).items():
        out[i] = vector
    return (jnp.stack(results), jnp.stack(input_grads), *out)


def solution(mesh):
    clips = P(("shard", "rep"), None, None)
    weights = tuple(P("shard", None) if i in WEIGHTS else P("shard") for i in range(15))
    return jax.shard_map(
        functools.partial(per_device, mesh.shape["shard"], mesh.shape["rep"]),
        mesh=mesh,
        in_specs=(clips, clips) + weights,
        out_specs=(clips, clips) + weights,
        check_vma=False,
    )
```
